32 devices in a mesh: user: 8 (over y, x, core), item: 4 (over z).
Axes of the slice: x: 2, y: 2, z: 4, core: 2. Of those that a mesh axis runs over, the one named last changes fastest.
Arguments:
- user_factors: float32 [4096, 256], P('user'), may hold values from -1.5 to 1.5
- item_factors: float32 [32768, 256], P(('user', 'item')), may hold values from -1.5 to 1.5
- feedback: bfloat16 [128, 4096, 128], P('item', 'user'), may hold values from 0 to 1
- item_pick: int32 [32, 32], replicated, may hold values from 0 to 7, as said below
- user_noise: float32 [4096, 256], P('user'), may hold values from -6 to 6
- item_noise: float32 [32768, 256], P(('user', 'item')), may hold values from -6 to 6
Outputs:
- new_user: float32 [4096, 256], P('user')
- new_item: float32 [32768, 256], P(('user', 'item'))
The draws below stay inside these ranges and needn't reach their ends.
Inputs may be any that keep to these rules, and one draw needn't show every extreme that they name: For every owner o and every user slab u, the 4 entries item_pick[u * 4 + i, o] are distinct, so that no tile appears twice.
All inputs are finite; a program needn't handle non-finite values.
Results may differ from the reference program's by a relative error of at most 0.00058.
Values may be sent and summed in bfloat16 or wider, within the bound.
A program may use at most 192 MiB of HBM per device.

```python
import math
import jax
import jax.numpy as jnp
from jax import lax

RANK = 256
TILE = 128
UB_DEV = 4
IB_DEV = 8
USERS = 4096
ITEMS = 32768
N_ITEM = 4
DEVICES = 32


def draw_item_pick(key, part):
    user_rows = DEVICES // N_ITEM
    ranking = jax.random.randint(key, (user_rows, DEVICES, IB_DEV), 0, 1 << 20) * IB_DEV + jnp.arange(IB_DEV, dtype=jnp.int32)
    picked = jnp.argsort(ranking, axis=-1)[:, :, :N_ITEM]
    return jnp.transpose(picked, (0, 2, 1)).reshape(DEVICES, DEVICES).astype(jnp.int32)


def level_of(own_key, dims, split, smallest, largest):
    def one(axis_at, shards_of):
        draws = jax.random.uniform(jax.random.fold_in(jax.random.fold_in(own_key, 6), axis_at), (shards_of,), jnp.float32, smallest / len(split), largest / len(split))
        return jnp.repeat(jnp.exp(draws), dims[axis_at] // shards_of).reshape((-1,) + (1,) * (len(dims) - axis_at - 1))

    factor_of = one(*split[0])
    for cut in split[1:]:
        factor_of = factor_of * one(*cut)
    return factor_of


def scatter_about(own_key, shape, deviation, reach, shards=(), kind=jnp.bfloat16):
    loudness = level_of(own_key, shape, shards, -0.22, 0.18) if shards else 1.0
    values = jax.random.normal(own_key, shape, jnp.float32) * deviation * loudness
    return jnp.minimum(jnp.maximum(values, -reach), reach).astype(kind)


def setup_inputs(seed: int = 0) -> dict:
    key_of = jax.random.split(jax.random.key(seed), 7)
    user_factors = scatter_about(key_of[0], (USERS, RANK), 0.25, 1.5, ((0, 8),), jnp.float32)
    item_factors = scatter_about(key_of[1], (ITEMS, RANK), 0.25, 1.5, ((0, 32),), jnp.float32)
    feedback = jnp.clip(1.0 * jax.random.uniform(key_of[2], (N_ITEM * DEVICES, USERS, TILE), jnp.float32) ** level_of(key_of[2], (N_ITEM * DEVICES, USERS, TILE), ((0, 4), (1, 8)), -0.2, 0.2), 0.0, 1.0).astype(jnp.bfloat16)
    item_pick = draw_item_pick(jax.random.fold_in(key_of[6], 71), 0)
    user_noise = scatter_about(key_of[4], (USERS, RANK), 1.0, 6.0, ((0, 8),), jnp.float32)
    item_noise = scatter_about(key_of[5], (ITEMS, RANK), 1.0, 6.0, ((0, 32),), jnp.float32)
    return {"user_factors": user_factors, "item_factors": item_factors, "feedback": feedback, "item_pick": item_pick, "user_noise": user_noise, "item_noise": item_noise}


step_size = 0.01
item_step = 0.1
prior_weight = 1.0
noise_scale = math.sqrt(0.02)
item_noise_scale = math.sqrt(0.2)

def reference(user_factors, item_factors, feedback, item_pick, user_noise, item_noise):
    slab_rows = UB_DEV * TILE
    item_half = item_factors.astype(jnp.bfloat16).reshape(IB_DEV * DEVICES, TILE, RANK)
    owners = jnp.arange(DEVICES, dtype=jnp.int32) * IB_DEV

    def one_device(totals, device):
        user_row = (device // N_ITEM).astype(jnp.int32)
        item_col = (device % N_ITEM).astype(jnp.int32)
        user_slab = lax.dynamic_slice_in_dim(user_factors, user_row * slab_rows, slab_rows, 0).astype(jnp.bfloat16)
        tiles = lax.dynamic_slice(feedback, (item_col * DEVICES, user_row * slab_rows, jnp.int32(0)), (DEVICES, slab_rows, TILE))
        blocks = (owners + item_pick[device]).astype(jnp.int32)
        fetched = item_half[blocks]
        scores = jnp.einsum('uk,ntk->nut', user_slab.astype(jnp.float32), fetched.astype(jnp.float32))
        residual = (jax.nn.sigmoid(scores) - tiles.astype(jnp.float32)).astype(jnp.bfloat16)
        user_grad = jnp.einsum('nut,ntk->uk', residual.astype(jnp.float32), fetched.astype(jnp.float32))
        item_part = jnp.einsum('nut,uk->ntk', residual.astype(jnp.float32), user_slab.astype(jnp.float32))
        totals = totals.at[blocks].add(item_part)
        return (totals, user_grad)
    start_grad = jnp.zeros((IB_DEV * DEVICES, TILE, RANK), jnp.float32)
    item_grad, user_parts = lax.scan(one_device, start_grad, jnp.arange(DEVICES, dtype=jnp.int32))
    user_grad = lax.optimization_barrier(jnp.sum(user_parts.reshape(DEVICES // N_ITEM, N_ITEM, slab_rows, RANK), axis=1)).reshape(USERS, RANK)
    new_user = user_factors - step_size * (user_grad + prior_weight * user_factors) + noise_scale * user_noise
    new_item = item_factors - item_step * (item_grad.reshape(ITEMS, RANK) + prior_weight * item_factors) + item_noise_scale * item_noise
    return (new_user, new_item)
```

```python
import math

import jax
import jax.numpy as jnp
from jax import lax
from jax.sharding import PartitionSpec as P

step_size = 0.01
item_step = 0.1
prior_weight = 1.0
noise_scale = math.sqrt(0.02)
item_noise_scale = math.sqrt(0.2)


def local(user_factors, item_factors, feedback, item_pick, user_noise, item_noise):
    devices = lax.axis_size(("user", "item"))
    own_index = lax.axis_index(("user", "item"))
    tile_size = feedback.shape[2]
    rank_width = item_factors.shape[1]
    held_blocks = item_factors.shape[0] // tile_size
    item_half = item_factors.astype(jnp.bfloat16).reshape(held_blocks, tile_size, rank_width)
    wanted = lax.dynamic_slice_in_dim(item_pick, own_index, 1, 1)[:, 0]
    outgoing = jnp.take(item_half, wanted, axis=0)
    arrived = lax.all_to_all(outgoing, ("user", "item"), split_axis=0, concat_axis=0, tiled=True)
    user_slab = user_factors.astype(jnp.bfloat16)
    scores = jnp.einsum("uk,ntk->nut", user_slab, arrived, preferred_element_type=jnp.float32)
    residual = (jax.nn.sigmoid(scores) - feedback.astype(jnp.float32)).astype(jnp.bfloat16)
    user_grad = jnp.einsum("nut,ntk->uk", residual, arrived, preferred_element_type=jnp.float32)
    item_part = jnp.einsum("nut,uk->ntk", residual, user_slab, preferred_element_type=jnp.float32)
    returned = lax.all_to_all(
        item_part.astype(jnp.float16), ("user", "item"), split_axis=0, concat_axis=0, tiled=True
    ).astype(jnp.float32).reshape(devices, tile_size * rank_width)
    selector = (wanted[None, :] == jnp.arange(held_blocks, dtype=jnp.int32)[:, None]).astype(
        jnp.float32
    )
    item_grad = jnp.dot(
        selector, returned, precision=lax.Precision.HIGHEST, preferred_element_type=jnp.float32
    ).reshape(item_factors.shape)
    new_item = (
        item_factors
        - item_step * (item_grad + prior_weight * item_factors)
        + item_noise_scale * item_noise
    )
    grad_total = lax.psum(user_grad, "item")
    new_user = (
        user_factors
        - step_size * (grad_total + prior_weight * user_factors)
        + noise_scale * user_noise
    )
    return (new_user, new_item)


def solution(mesh):
    in_specs = (
        P("user", None),
        P(("user", "item"), None),
        P("item", "user", None),
        P(),
        P("user", None),
        P(("user", "item"), None),
    )
    out_specs = (P("user", None), P(("user", "item"), None))
    return jax.shard_map(local, mesh=mesh, in_specs=in_specs, out_specs=out_specs, check_vma=False)
```

```python
import functools
import math

import jax
import jax.numpy as jnp
from jax import lax
from jax.experimental import pallas as pl
from jax.experimental.pallas import tpu as pltpu
from jax.sharding import PartitionSpec as P

step_size = 0.01
item_step = 0.1
prior_weight = 1.0
noise_scale = math.sqrt(0.02)
item_noise_scale = math.sqrt(0.2)

FACTOR_BOUND = 1.5
LEVELS = 32766.0
PAD = 16


def encode(ref, value, unit):
    rows = value.shape[0]
    largest = jnp.max(jnp.abs(value), axis=0, keepdims=True)
    count = jnp.floor(largest * (1.0 / (LEVELS * unit))) + 1.0
    inverse = 1.0 / (count * unit)
    ref[pl.ds(0, rows), :] = jnp.round(value * inverse).astype(jnp.int32).astype(jnp.int16)
    ref[pl.ds(rows, PAD), :] = jnp.broadcast_to(count, (PAD, value.shape[1])).astype(jnp.int32).astype(jnp.int16)


def decode(ref, weight):
    rows = ref.shape[0] - PAD
    count = ref[pl.ds(rows, PAD), :].astype(jnp.float32)[0:1]
    return ref[pl.ds(0, rows), :].astype(jnp.float32) * (count * weight)


def kernel(
    U, Z, pick, items, user, feedback, item_out, user_out, *scratch
):
    zbufs = scratch[: 2 * (Z - 1)]
    (og, arr, gs, gr, cs, cr, crd, fb, us, ur, ugs, ugr, ug, zsend, zrecv, isend, irecv, gsend, grecv,
     csend, crecv, cdrecv, fsem, usend, urecv, vsend, vrecv) = scratch[2 * (Z - 1):]
    B, T, K = items.shape
    N = user.shape[0]
    piece = N // Z
    me = lax.axis_index("user")
    z = lax.axis_index("item")
    item_unit = N * FACTOR_BOUND * U / LEVELS / 32000.0
    user_unit = U * Z * T * FACTOR_BOUND * Z / LEVELS / 32000.0

    def far(axis, to, src, dst, ssem, rsem):
        return pltpu.make_async_remote_copy(
            src_ref=src, dst_ref=dst, send_sem=ssem, recv_sem=rsem,
            device_id={axis: to}, device_id_type=pl.DeviceIdType.MESH)

    barrier = pltpu.get_barrier_semaphore()

    def greet_user(j, c):
        pl.semaphore_signal(barrier, inc=1, device_id={"user": lax.rem(me + j, U)}, device_id_type=pl.DeviceIdType.MESH)
        return c

    lax.fori_loop(1, U, greet_user, 0)
    for j in range(1, Z):
        pl.semaphore_signal(barrier, inc=1, device_id={"item": lax.rem(z + j, Z)}, device_id_type=pl.DeviceIdType.MESH)
    pl.semaphore_wait(barrier, U - 1 + Z - 1)

    def zcopy(d, way):
        src = items if d == 1 else zbufs[2 * (d - 2) + way]
        k = 2 * (d - 1) + way
        return far("item", z + (1 if way == 0 else -1), src, zbufs[k], zsend.at[k], zrecv.at[k])

    def can_send(d, way):
        return (z - (d - 1) >= 0) & (z + 1 < Z) if way == 0 else (z + (d - 1) < Z) & (z >= 1)

    def comes(d, way):
        return z - d >= 0 if way == 0 else z + d < Z

    for way in (0, 1):
        pl.when(can_send(1, way))(lambda way=way: zcopy(1, way).start())

    ug[...] = jnp.zeros_like(ug)

    def icopy(p, to, src):
        return far("user", to, og.at[p, to], arr.at[p, src], isend.at[p, to], irecv.at[p, src])

    def spread(p, blocks):
        def one(j, c):
            to = lax.rem(me + j, U)
            og[p, to] = blocks[pick[to * Z + z, me * Z + p]]
            icopy(p, to, me).start()
            return c
        lax.fori_loop(1, U, one, 0)
        arr[p, me] = blocks[pick[me * Z + z, me * Z + p]]

    def gcopy(p, to, src):
        return far("user", to, gs.at[p, to], gr.at[p, src], gsend.at[p, to], grecv.at[p, src])

    def fcopy(p, pair, slot):
        return pltpu.make_async_copy(feedback.at[pl.ds(2 * pair, 2), p], fb.at[slot], fsem.at[slot])

    pairs = U // 2

    def pair_of(j):
        return lax.rem(me // 2 + 1 + j, pairs)

    def compute(p):
        fcopy(p, pair_of(0), 0).start()

        def one(j, c):
            pair = pair_of(j)
            slot = lax.rem(j, 2)

            @pl.when(j + 1 < pairs)
            def _():
                fcopy(p, pair_of(j + 1), 1 - slot).start()

            for t in range(2):
                o = 2 * pair + t
                pl.when(o != me)(lambda o=o: icopy(p, me, o).wait_recv())
            fcopy(p, pair, slot).wait()
            tile = arr[p, pl.ds(2 * pair, 2)].reshape(2 * T, K)
            scores = lax.dot_general(user[...], tile, (((1,), (1,)), ((), ())), preferred_element_type=jnp.float32)
            target = jnp.concatenate([fb[slot, 0], fb[slot, 1]], axis=1).astype(jnp.float32)
            residual = (0.5 * jnp.tanh(0.5 * scores) + (0.5 - target)).astype(jnp.bfloat16)
            part = lax.dot_general(residual, user[...], (((0,), (0,)), ((), ())), preferred_element_type=jnp.float32)
            for t in range(2):
                o = 2 * pair + t
                value = part[t * T:(t + 1) * T]

                @pl.when(o != me)
                def _():
                    encode(gs.at[p, o], value, item_unit)
                    gcopy(p, o, me).start()

                @pl.when(o == me)
                def _():
                    encode(gr.at[p, me], value, item_unit)
            ug[...] += jnp.dot(residual, tile, preferred_element_type=jnp.float32)
            return c

        lax.fori_loop(0, pairs, one, 0)

    def dense(p, b):
        def one(u, acc):
            weight = jnp.where(pick[u * Z + z, me * Z + p] == b, item_unit, 0.0).astype(jnp.float32)
            return acc + decode(gr.at[p, u], weight)
        return lax.fori_loop(0, U, one, jnp.zeros((T, K), jnp.float32))

    def await_grads(p):
        def one(j, c):
            gcopy(p, me, lax.rem(me + j, U)).wait_recv()
            return c
        lax.fori_loop(1, U, one, 0)

    def chain(p, way, relay):
        await_grads(p)
        to = z + (1 if way == 0 else -1)

        def one(b, c):
            total = dense(p, b)
            if relay:
                far("item", z, cs.at[p, b], cr.at[p, b], csend.at[p, b], crecv.at[p, b]).wait_recv()
                total = total + decode(cr.at[p, b], item_unit)
            encode(cs.at[p, b], total, item_unit)
            if way == 0:
                far("item", to, cs.at[p, b], cr.at[p, b], csend.at[p, b], crecv.at[p, b]).start()
            else:
                @pl.when(to == p)
                def _():
                    far("item", to, cs.at[p, b], crd.at[b], csend.at[p, b], cdrecv.at[b]).start()

                @pl.when(to != p)
                def _():
                    far("item", to, cs.at[p, b], cr.at[p, b], csend.at[p, b], crecv.at[p, b]).start()
            return c
        lax.fori_loop(0, B, one, 0)

    def plane(d, way):
        return z - d if way == 0 else z + d

    def start_chain(d, way):
        out = 1 - way
        edge = z == 0 if out == 0 else z == Z - 1

        @pl.when(comes(d, way) & edge)
        def _():
            chain(plane(d, way), out, False)

    steps = [(d, way) for d in range(1, Z) for way in (0, 1)]
    spread(z, items)
    last = None
    older = None
    compute_own = True
    for d in range(1, Z):
        for way in (0, 1):
            @pl.when(comes(d, way))
            def _(d=d, way=way):
                zcopy(d, way).wait_recv()
                if d + 1 < Z:
                    pl.when(can_send(d + 1, way))(lambda: zcopy(d + 1, way).start())
                spread(plane(d, way), zbufs[2 * (d - 1) + way])
        if d == 1:
            compute(z)
        else:
            for way in (0, 1):
                pl.when(comes(d - 1, way))(lambda d=d, way=way: compute(plane(d - 1, way)))
        if d > 2:
            for way in (0, 1):
                start_chain(d - 2, way)
    for way in (0, 1):
        pl.when(comes(Z - 1, way))(lambda way=way: compute(plane(Z - 1, way)))

    def ucopy(to, src):
        return far("item", to, us.at[to], ur.at[src], usend.at[to], urecv.at[src])

    for j in range(1, Z):
        to = lax.rem(z + j, Z)
        encode(us.at[to], ug[pl.ds(pl.multiple_of(to * piece, piece), piece), :], user_unit)
        ucopy(to, z).start()
    for d in range(max(Z - 2, 1), Z):
        for way in (0, 1):
            start_chain(d, way)

    def vcopy(to, src, j):
        return far("item", to, ugs, ugr.at[src], vsend.at[j], vrecv.at[src])

    total = ug[pl.ds(pl.multiple_of(z * piece, piece), piece), :]
    for j in range(1, Z):
        src = lax.rem(z + j, Z)
        ucopy(z, src).wait_recv()
        total = total + decode(ur.at[src], user_unit)
    encode(ugs, total, user_unit)
    for j in range(1, Z):
        vcopy(lax.rem(z + j, Z), z, j - 1).start()
    user_out[pl.ds(pl.multiple_of(z * piece, piece), piece), :] = decode(ugs, user_unit)

    for d in range(1, Z):
        pl.when((z > 0) & (z + d < Z))(lambda d=d: chain(z + d, 0, True))
    for d in range(1, Z):
        pl.when((z < Z - 1) & (z - d >= 0))(lambda d=d: chain(z - d, 1, True))

    await_grads(z)

    def finish(b, c):
        item_out[b] = dense(z, b)

        @pl.when(z > 0)
        def _():
            far("item", z, cs.at[z, b], cr.at[z, b], csend.at[z, b], crecv.at[z, b]).wait_recv()
            item_out[b] += decode(cr.at[z, b], item_unit)

        @pl.when(z < Z - 1)
        def _():
            far("item", z, cs.at[z, b], crd.at[b], csend.at[z, b], cdrecv.at[b]).wait_recv()
            item_out[b] += decode(crd.at[b], item_unit)
        return c

    lax.fori_loop(0, B, finish, 0)

    for j in range(1, Z):
        src = lax.rem(z + j, Z)
        vcopy(z, src, j - 1).wait_recv()
        user_out[pl.ds(pl.multiple_of(src * piece, piece), piece), :] = decode(ugr.at[src], user_unit)

    for d in range(1, Z):
        for way in (0, 1):
            pl.when(can_send(d, way))(lambda d=d, way=way: zcopy(d, way).wait_send())

    def drain(j, c):
        to = lax.rem(me + j, U)
        for p in range(Z):
            icopy(p, to, me).wait_send()
            gcopy(p, to, me).wait_send()
        return c

    lax.fori_loop(1, U, drain, 0)
    for j in range(1, Z):
        to = lax.rem(z + j, Z)
        ucopy(to, z).wait_send()
        vcopy(to, z, j - 1).wait_send()

        def drained(b, c):
            far("item", z, cs.at[to, b], cr.at[to, b], csend.at[to, b], crecv.at[to, b]).wait_send()
            return c
        lax.fori_loop(0, B, drained, 0)


def exchange(pick, items, user, feedback, U, Z):
    B, T, K = items.shape
    N = user.shape[0]
    piece = N // Z
    coded = T + PAD
    dma = pltpu.SemaphoreType.DMA
    i16 = jnp.int16
    vmem = pl.BlockSpec(memory_space=pltpu.VMEM)
    return pl.pallas_call(
        functools.partial(kernel, U, Z),
        out_shape=(jax.ShapeDtypeStruct((B, T, K), jnp.float32), jax.ShapeDtypeStruct((N, K), jnp.float32)),
        in_specs=[pl.BlockSpec(memory_space=pltpu.SMEM), vmem, vmem, pl.BlockSpec(memory_space=pl.ANY)],
        out_specs=(vmem, vmem),
        scratch_shapes=[pltpu.VMEM((B, T, K), jnp.bfloat16)] * (2 * (Z - 1)) + [
            pltpu.VMEM((Z, U, T, K), jnp.bfloat16),
            pltpu.VMEM((Z, U, T, K), jnp.bfloat16),
            pltpu.VMEM((Z, U, coded, K), i16),
            pltpu.VMEM((Z, U, coded, K), i16),
            pltpu.VMEM((Z, B, coded, K), i16),
            pltpu.VMEM((Z, B, coded, K), i16),
            pltpu.VMEM((B, coded, K), i16),
            pltpu.VMEM((2, 2, N, T), jnp.bfloat16),
            pltpu.VMEM((Z, piece + PAD, K), i16),
            pltpu.VMEM((Z, piece + PAD, K), i16),
            pltpu.VMEM((piece + PAD, K), i16),
            pltpu.VMEM((Z, piece + PAD, K), i16),
            pltpu.VMEM((N, K), jnp.float32),
            dma((2 * (Z - 1),)), dma((2 * (Z - 1),)),
            dma((Z, U)), dma((Z, U)), dma((Z, U)), dma((Z, U)),
            dma((Z, B)), dma((Z, B)), dma((B,)),
            dma((2,)),
            dma((Z,)), dma((Z,)), dma((Z,)), dma((Z,)),
        ],
        compiler_params=pltpu.CompilerParams(
            collective_id=0, has_side_effects=True, vmem_limit_bytes=63 * 2**20),
    )(pick, items, user, feedback)


def local(user_factors, item_factors, feedback, item_pick, user_noise, item_noise):
    U, Z = lax.axis_size("user"), lax.axis_size("item")
    tile, rank = feedback.shape[2], item_factors.shape[1]
    held = item_factors.shape[0] // tile
    items = item_factors.astype(jnp.bfloat16).reshape(held, tile, rank)
    item_grad, user_grad = exchange(
        item_pick, items, user_factors.astype(jnp.bfloat16),
        feedback.reshape(U, Z, feedback.shape[1], tile), U, Z)
    item_grad = item_grad.reshape(item_factors.shape)
    new_item = item_factors - item_step * (item_grad + prior_weight * item_factors) + item_noise_scale * item_noise
    new_user = user_factors - step_size * (user_grad + prior_weight * user_factors) + noise_scale * user_noise
    return (new_user, new_item)


def solution(mesh):
    in_specs = (
        P("user", None),
        P(("user", "item"), None),
        P("item", "user", None),
        P(),
        P("user", None),
        P(("user", "item"), None),
    )
    out_specs = (P("user", None), P(("user", "item"), None))
    return jax.shard_map(local, mesh=mesh, in_specs=in_specs, out_specs=out_specs, check_vma=False)
```

```python
import functools
import math

import jax
import jax.numpy as jnp
from jax import lax
from jax.experimental import pallas as pl
from jax.experimental.pallas import tpu as pltpu
from jax.sharding import PartitionSpec as P

step_size = 0.01
item_step = 0.1
prior_weight = 1.0
noise_scale = math.sqrt(0.02)
item_noise_scale = math.sqrt(0.2)

FACTOR_BOUND = 1.5
LEVELS = 32766.0
PAD = 16


def encode(ref, value, unit):
    rows = value.shape[0]
    largest = jnp.max(jnp.abs(value), axis=0, keepdims=True)
    count = jnp.floor(largest * (1.0 / (LEVELS * unit))) + 1.0
    inverse = 1.0 / (count * unit)
    ref[pl.ds(0, rows), :] = jnp.round(value * inverse).astype(jnp.int32).astype(jnp.int16)
    ref[pl.ds(rows, PAD), :] = jnp.broadcast_to(count, (PAD, value.shape[1])).astype(jnp.int32).astype(jnp.int16)


def decode(ref, weight):
    rows = ref.shape[0] - PAD
    count = ref[pl.ds(rows, PAD), :].astype(jnp.float32)[0:1]
    return ref[pl.ds(0, rows), :].astype(jnp.float32) * (count * weight)


def kernel(
    U, Z, pick, items, user, feedback, item_out, user_out, *scratch
):
    zbufs = scratch[: 2 * (Z - 1)]
    (og, arr, gs, gr, cs, cr, crd, fb, us, ur, ugs, ugr, ug, zsend, zrecv, isend, irecv, gsend, grecv,
     csend, crecv, cdrecv, fsem, usend, urecv, vsend, vrecv) = scratch[2 * (Z - 1):]
    B, T, K = items.shape
    N = user.shape[0]
    piece = N // Z
    me = lax.axis_index("user")
    z = lax.axis_index("item")
    item_unit = N * FACTOR_BOUND * U / LEVELS / 32000.0
    user_unit = U * Z * T * FACTOR_BOUND * Z / LEVELS / 32000.0

    def far(axis, to, src, dst, ssem, rsem):
        return pltpu.make_async_remote_copy(
            src_ref=src, dst_ref=dst, send_sem=ssem, recv_sem=rsem,
            device_id={axis: to}, device_id_type=pl.DeviceIdType.MESH)

    barrier = pltpu.get_barrier_semaphore()

    def greet_user(j, c):
        pl.semaphore_signal(barrier, inc=1, device_id={"user": lax.rem(me + j, U)}, device_id_type=pl.DeviceIdType.MESH)
        return c

    lax.fori_loop(1, U, greet_user, 0)
    for j in range(1, Z):
        pl.semaphore_signal(barrier, inc=1, device_id={"item": lax.rem(z + j, Z)}, device_id_type=pl.DeviceIdType.MESH)
    pl.semaphore_wait(barrier, U - 1 + Z - 1)

    def zcopy(d, way):
        src = items if d == 1 else zbufs[2 * (d - 2) + way]
        k = 2 * (d - 1) + way
        return far("item", z + (1 if way == 0 else -1), src, zbufs[k], zsend.at[k], zrecv.at[k])

    def can_send(d, way):
        return (z - (d - 1) >= 0) & (z + 1 < Z) if way == 0 else (z + (d - 1) < Z) & (z >= 1)

    def comes(d, way):
        return z - d >= 0 if way == 0 else z + d < Z

    for way in (0, 1):
        pl.when(can_send(1, way))(lambda way=way: zcopy(1, way).start())

    ug[...] = jnp.zeros_like(ug)

    def icopy(p, to, src):
        return far("user", to, og.at[p, to], arr.at[p, src], isend.at[p, to], irecv.at[p, src])

    def spread(p, blocks):
        def one(j, c):
            to = lax.rem(me + j, U)
            og[p, to] = blocks[pick[to * Z + z, me * Z + p]]
            icopy(p, to, me).start()
            return c
        lax.fori_loop(1, U, one, 0)
        arr[p, me] = blocks[pick[me * Z + z, me * Z + p]]

    def gcopy(p, to, src):
        return far("user", to, gs.at[p, to], gr.at[p, src], gsend.at[p, to], grecv.at[p, src])

    def fcopy(p, pair, slot):
        return pltpu.make_async_copy(feedback.at[pl.ds(2 * pair, 2), p], fb.at[slot], fsem.at[slot])

    pairs = U // 2

    def pair_of(j):
        return lax.rem(me // 2 + 1 + j, pairs)

    def compute(p):
        fcopy(p, pair_of(0), 0).start()

        def one(j, c):
            pair = pair_of(j)
            slot = lax.rem(j, 2)

            @pl.when(j + 1 < pairs)
            def _():
                fcopy(p, pair_of(j + 1), 1 - slot).start()

            for t in range(2):
                o = 2 * pair + t
                pl.when(o != me)(lambda o=o: icopy(p, me, o).wait_recv())
            fcopy(p, pair, slot).wait()
            tile = arr[p, pl.ds(2 * pair, 2)].reshape(2 * T, K)
            scores = lax.dot_general(user[...], tile, (((1,), (1,)), ((), ())), preferred_element_type=jnp.float32)
            target = jnp.concatenate([fb[slot, 0], fb[slot, 1]], axis=1).astype(jnp.float32)
            residual = (0.5 * jnp.tanh(0.5 * scores) + (0.5 - target)).astype(jnp.bfloat16)
            part = lax.dot_general(residual, user[...], (((0,), (0,)), ((), ())), preferred_element_type=jnp.float32)
            for t in range(2):
                o = 2 * pair + t
                value = part[t * T:(t + 1) * T]

                @pl.when(o != me)
                def _():
                    encode(gs.at[p, o], value, item_unit)
                    gcopy(p, o, me).start()

                @pl.when(o == me)
                def _():
                    encode(gr.at[p, me], value, item_unit)
            ug[...] += jnp.dot(residual, tile, preferred_element_type=jnp.float32)
            return c

        lax.fori_loop(0, pairs, one, 0)

    def dense(p, b):
        def one(u, acc):
            weight = jnp.where(pick[u * Z + z, me * Z + p] == b, item_unit, 0.0).astype(jnp.float32)
            return acc + decode(gr.at[p, u], weight)
        return lax.fori_loop(0, U, one, jnp.zeros((T, K), jnp.float32))

    def await_grads(p):
        def one(j, c):
            gcopy(p, me, lax.rem(me + j, U)).wait_recv()
            return c
        lax.fori_loop(1, U, one, 0)

    def pass_on(p, b, way, relay):
        to = z + (1 if way == 0 else -1)
        total = dense(p, b)
        if relay:
            far("item", z, cs.at[p, b], cr.at[p, b], csend.at[p, b], crecv.at[p, b]).wait_recv()
            total = total + decode(cr.at[p, b], item_unit)
        encode(cs.at[p, b], total, item_unit)
        if way == 0:
            far("item", to, cs.at[p, b], cr.at[p, b], csend.at[p, b], crecv.at[p, b]).start()
        else:
            @pl.when(to == p)
            def _():
                far("item", to, cs.at[p, b], crd.at[b], csend.at[p, b], cdrecv.at[b]).start()

            @pl.when(to != p)
            def _():
                far("item", to, cs.at[p, b], cr.at[p, b], csend.at[p, b], crecv.at[p, b]).start()

    def chain(p, way):
        await_grads(p)

        def one(b, c):
            pass_on(p, b, way, False)
            return c
        lax.fori_loop(0, B, one, 0)

    def plane(d, way):
        return z - d if way == 0 else z + d

    def start_chain(d, way):
        out = 1 - way
        edge = z == 0 if out == 0 else z == Z - 1

        @pl.when(comes(d, way) & edge)
        def _():
            chain(plane(d, way), out)

    spread(z, items)
    compute(z)
    for d in range(1, Z):
        for way in (0, 1):
            @pl.when(comes(d, way))
            def _(d=d, way=way):
                zcopy(d, way).wait_recv()
                if d + 1 < Z:
                    pl.when(can_send(d + 1, way))(lambda: zcopy(d + 1, way).start())
                spread(plane(d, way), zbufs[2 * (d - 1) + way])
        if d > 1:
            for way in (0, 1):
                start_chain(d - 1, way)
        for way in (0, 1):
            pl.when(comes(d, way))(lambda d=d, way=way: compute(plane(d, way)))

    def ucopy(to, src):
        return far("item", to, us.at[to], ur.at[src], usend.at[to], urecv.at[src])

    for j in range(1, Z):
        to = lax.rem(z + j, Z)
        encode(us.at[to], ug[pl.ds(pl.multiple_of(to * piece, piece), piece), :], user_unit)
        ucopy(to, z).start()
    for way in (0, 1):
        start_chain(Z - 1, way)

    def vcopy(to, src, j):
        return far("item", to, ugs, ugr.at[src], vsend.at[j], vrecv.at[src])

    def share_users():
        total = ug[pl.ds(pl.multiple_of(z * piece, piece), piece), :]
        for j in range(1, Z):
            src = lax.rem(z + j, Z)
            ucopy(z, src).wait_recv()
            total = total + decode(ur.at[src], user_unit)
        encode(ugs, total, user_unit)
        for j in range(1, Z):
            vcopy(lax.rem(z + j, Z), z, j - 1).start()
        user_out[pl.ds(pl.multiple_of(z * piece, piece), piece), :] = decode(ugs, user_unit)

    inner = (z > 0) & (z < Z - 1)
    pl.when(inner)(lambda: [await_grads(lax.rem(z + j, Z)) for j in range(1, Z)] and None)

    def relay(r):
        def up(b):
            pl.when(z < r)(lambda: pass_on(r, b, 0, True))

        def down(b):
            pl.when(z > Z - 1 - r)(lambda: pass_on(Z - 1 - r, b, 1, True))

        def one(b, c):
            pl.when(2 * z < Z - 1)(lambda: up(b))
            down(b)
            pl.when(2 * z >= Z - 1)(lambda: up(b))
            return c
        lax.fori_loop(0, B, one, 0)

    for r in range(1, Z - 1):
        pl.when(inner)(lambda r=r: relay(r))
    share_users()
    pl.when(inner)(lambda: relay(Z - 1))

    await_grads(z)

    def finish(b, c):
        item_out[b] = dense(z, b)

        @pl.when(z > 0)
        def _():
            far("item", z, cs.at[z, b], cr.at[z, b], csend.at[z, b], crecv.at[z, b]).wait_recv()
            item_out[b] += decode(cr.at[z, b], item_unit)

        @pl.when(z < Z - 1)
        def _():
            far("item", z, cs.at[z, b], crd.at[b], csend.at[z, b], cdrecv.at[b]).wait_recv()
            item_out[b] += decode(crd.at[b], item_unit)
        return c

    lax.fori_loop(0, B, finish, 0)

    for j in range(1, Z):
        src = lax.rem(z + j, Z)
        vcopy(z, src, j - 1).wait_recv()
        user_out[pl.ds(pl.multiple_of(src * piece, piece), piece), :] = decode(ugr.at[src], user_unit)

    for d in range(1, Z):
        for way in (0, 1):
            pl.when(can_send(d, way))(lambda d=d, way=way: zcopy(d, way).wait_send())

    def drain(j, c):
        to = lax.rem(me + j, U)
        for p in range(Z):
            icopy(p, to, me).wait_send()
            gcopy(p, to, me).wait_send()
        return c

    lax.fori_loop(1, U, drain, 0)
    for j in range(1, Z):
        to = lax.rem(z + j, Z)
        ucopy(to, z).wait_send()
        vcopy(to, z, j - 1).wait_send()

        def drained(b, c):
            far("item", z, cs.at[to, b], cr.at[to, b], csend.at[to, b], crecv.at[to, b]).wait_send()
            return c
        lax.fori_loop(0, B, drained, 0)


def exchange(pick, items, user, feedback, U, Z):
    B, T, K = items.shape
    N = user.shape[0]
    piece = N // Z
    coded = T + PAD
    dma = pltpu.SemaphoreType.DMA
    i16 = jnp.int16
    vmem = pl.BlockSpec(memory_space=pltpu.VMEM)
    return pl.pallas_call(
        functools.partial(kernel, U, Z),
        out_shape=(jax.ShapeDtypeStruct((B, T, K), jnp.float32), jax.ShapeDtypeStruct((N, K), jnp.float32)),
        in_specs=[pl.BlockSpec(memory_space=pltpu.SMEM), vmem, vmem, pl.BlockSpec(memory_space=pl.ANY)],
        out_specs=(vmem, vmem),
        scratch_shapes=[pltpu.VMEM((B, T, K), jnp.bfloat16)] * (2 * (Z - 1)) + [
            pltpu.VMEM((Z, U, T, K), jnp.bfloat16),
            pltpu.VMEM((Z, U, T, K), jnp.bfloat16),
            pltpu.VMEM((Z, U, coded, K), i16),
            pltpu.VMEM((Z, U, coded, K), i16),
            pltpu.VMEM((Z, B, coded, K), i16),
            pltpu.VMEM((Z, B, coded, K), i16),
            pltpu.VMEM((B, coded, K), i16),
            pltpu.VMEM((2, 2, N, T), jnp.bfloat16),
            pltpu.VMEM((Z, piece + PAD, K), i16),
            pltpu.VMEM((Z, piece + PAD, K), i16),
            pltpu.VMEM((piece + PAD, K), i16),
            pltpu.VMEM((Z, piece + PAD, K), i16),
            pltpu.VMEM((N, K), jnp.float32),
            dma((2 * (Z - 1),)), dma((2 * (Z - 1),)),
            dma((Z, U)), dma((Z, U)), dma((Z, U)), dma((Z, U)),
            dma((Z, B)), dma((Z, B)), dma((B,)),
            dma((2,)),
            dma((Z,)), dma((Z,)), dma((Z,)), dma((Z,)),
        ],
        compiler_params=pltpu.CompilerParams(
            collective_id=0, has_side_effects=True, vmem_limit_bytes=63 * 2**20),
    )(pick, items, user, feedback)


def local(user_factors, item_factors, feedback, item_pick, user_noise, item_noise):
    U, Z = lax.axis_size("user"), lax.axis_size("item")
    tile, rank = feedback.shape[2], item_factors.shape[1]
    held = item_factors.shape[0] // tile
    items = item_factors.astype(jnp.bfloat16).reshape(held, tile, rank)
    item_grad, user_grad = exchange(
        item_pick, items, user_factors.astype(jnp.bfloat16),
        feedback.reshape(U, Z, feedback.shape[1], tile), U, Z)
    item_grad = item_grad.reshape(item_factors.shape)
    new_item = item_factors - item_step * (item_grad + prior_weight * item_factors) + item_noise_scale * item_noise
    new_user = user_factors - step_size * (user_grad + prior_weight * user_factors) + noise_scale * user_noise
    return (new_user, new_item)


def solution(mesh):
    in_specs = (
        P("user", None),
        P(("user", "item"), None),
        P("item", "user", None),
        P(),
        P("user", None),
        P(("user", "item"), None),
    )
    out_specs = (P("user", None), P(("user", "item"), None))
    return jax.shard_map(local, mesh=mesh, in_specs=in_specs, out_specs=out_specs, check_vma=False)
```

```python
import functools
import math

import jax
import jax.numpy as jnp
from jax import lax
from jax.experimental import pallas as pl
from jax.experimental.pallas import tpu as pltpu
from jax.sharding import PartitionSpec as P

step_size = 0.01
item_step = 0.1
prior_weight = 1.0
noise_scale = math.sqrt(0.02)
item_noise_scale = math.sqrt(0.2)

FACTOR_BOUND = 1.5
LEVELS = 32766.0
PAD = 8


def encode(ref, value, unit):
    rows = value.shape[0]
    largest = jnp.max(jnp.abs(value), axis=0, keepdims=True)
    count = jnp.floor(largest * (1.0 / (LEVELS * unit))) + 1.0
    inverse = 1.0 / (count * unit)
    ref[pl.ds(0, rows), :] = jnp.round(value * inverse).astype(jnp.int32).astype(jnp.int16)
    ref[pl.ds(rows, PAD), :] = jnp.broadcast_to(count, (PAD, value.shape[1])).astype(jnp.int32).astype(jnp.int16)


def decode(ref, weight):
    rows = ref.shape[0] - PAD
    count = ref[pl.ds(rows, PAD), :].astype(jnp.float32)[0:1]
    return ref[pl.ds(0, rows), :].astype(jnp.float32) * (count * weight)


def kernel(
    U, Z, pick, items_wide, user_wide, feedback, item_out, user_out, *scratch
):
    zbufs = scratch[: 2 * (Z - 1)]
    (items, user, og, arr, gs, gr, cs, cr, crd, fb, us, ur, ugs, ugr, ug, zsend, zrecv, isend, irecv, gsend, grecv,
     csend, crecv, cdrecv, fsem, usend, urecv, vsend, vrecv) = scratch[2 * (Z - 1):]
    B, T, K = items.shape
    N = user.shape[0]
    piece = N // Z
    me = lax.axis_index("user")
    z = lax.axis_index("item")
    item_unit = N * FACTOR_BOUND * U / LEVELS / 32000.0
    user_unit = U * Z * T * FACTOR_BOUND * Z / LEVELS / 32000.0

    def far(axis, to, src, dst, ssem, rsem):
        return pltpu.make_async_remote_copy(
            src_ref=src, dst_ref=dst, send_sem=ssem, recv_sem=rsem,
            device_id={axis: to}, device_id_type=pl.DeviceIdType.MESH)

    barrier = pltpu.get_barrier_semaphore()

    items[...] = items_wide[...].astype(jnp.bfloat16)

    def greet_user(j, c):
        pl.semaphore_signal(barrier, inc=1, device_id={"user": lax.rem(me + j, U)}, device_id_type=pl.DeviceIdType.MESH)
        return c

    lax.fori_loop(1, U, greet_user, 0)
    for j in range(1, Z):
        pl.semaphore_signal(barrier, inc=1, device_id={"item": lax.rem(z + j, Z)}, device_id_type=pl.DeviceIdType.MESH)
    pl.semaphore_wait(barrier, U - 1 + Z - 1)

    def zcopy(d, way):
        src = items if d == 1 else zbufs[2 * (d - 2) + way]
        k = 2 * (d - 1) + way
        return far("item", z + (1 if way == 0 else -1), src, zbufs[k], zsend.at[k], zrecv.at[k])

    def can_send(d, way):
        return (z - (d - 1) >= 0) & (z + 1 < Z) if way == 0 else (z + (d - 1) < Z) & (z >= 1)

    def comes(d, way):
        return z - d >= 0 if way == 0 else z + d < Z

    for way in (0, 1):
        pl.when(can_send(1, way))(lambda way=way: zcopy(1, way).start())

    user[...] = user_wide[...].astype(jnp.bfloat16)
    ug[...] = jnp.zeros_like(ug)

    def icopy(p, to, src):
        return far("user", to, og.at[p, to], arr.at[p, src], isend.at[p, to], irecv.at[p, src])

    def spread(p, blocks):
        def one(j, c):
            to = lax.rem(me + j, U)
            og[p, to] = blocks[pick[to * Z + z, me * Z + p]]
            icopy(p, to, me).start()
            return c
        lax.fori_loop(1, U, one, 0)
        arr[p, me] = blocks[pick[me * Z + z, me * Z + p]]

    def gcopy(p, to, src):
        return far("user", to, gs.at[p, to], gr.at[p, src], gsend.at[p, to], grecv.at[p, src])

    def fcopy(p, pair, slot):
        return pltpu.make_async_copy(feedback.at[pl.ds(2 * pair, 2), p], fb.at[slot], fsem.at[slot])

    pairs = U // 2

    def pair_of(j):
        return lax.rem(me // 2 + pairs - j, pairs)

    def compute(p):
        fcopy(p, pair_of(0), 0).start()

        def one(j, c):
            pair = pair_of(j)
            slot = lax.rem(j, 2)

            @pl.when(j + 1 < pairs)
            def _():
                fcopy(p, pair_of(j + 1), 1 - slot).start()

            for t in range(2):
                o = 2 * pair + t
                pl.when(o != me)(lambda o=o: icopy(p, me, o).wait_recv())
            fcopy(p, pair, slot).wait()
            tile = arr[p, pl.ds(2 * pair, 2)].reshape(2 * T, K)
            scores = lax.dot_general(user[...], tile, (((1,), (1,)), ((), ())), preferred_element_type=jnp.float32)
            target = jnp.concatenate([fb[slot, 0], fb[slot, 1]], axis=1).astype(jnp.float32)
            residual = (0.5 * jnp.tanh(0.5 * scores) + (0.5 - target)).astype(jnp.bfloat16)
            part = lax.dot_general(residual, user[...], (((0,), (0,)), ((), ())), preferred_element_type=jnp.float32)
            for t in range(2):
                o = 2 * pair + t
                value = part[t * T:(t + 1) * T]

                @pl.when(o != me)
                def _():
                    encode(gs.at[p, o], value, item_unit)
                    gcopy(p, o, me).start()

                @pl.when(o == me)
                def _():
                    encode(gr.at[p, me], value, item_unit)
            ug[...] += jnp.dot(residual, tile, preferred_element_type=jnp.float32)
            return c

        lax.fori_loop(0, pairs, one, 0)

    def dense(p, b):
        def one(u, acc):
            weight = jnp.where(pick[u * Z + z, me * Z + p] == b, item_unit, 0.0).astype(jnp.float32)
            return acc + decode(gr.at[p, u], weight)
        return lax.fori_loop(0, U, one, jnp.zeros((T, K), jnp.float32))

    def await_grads(p):
        def one(j, c):
            gcopy(p, me, lax.rem(me + j, U)).wait_recv()
            return c
        lax.fori_loop(1, U, one, 0)

    def pass_on(p, b, way, relay):
        to = z + (1 if way == 0 else -1)
        total = dense(p, b)
        if relay:
            far("item", z, cs.at[p, b], cr.at[p, b], csend.at[p, b], crecv.at[p, b]).wait_recv()
            total = total + decode(cr.at[p, b], item_unit)
        encode(cs.at[p, b], total, item_unit)
        if way == 0:
            far("item", to, cs.at[p, b], cr.at[p, b], csend.at[p, b], crecv.at[p, b]).start()
        else:
            @pl.when(to == p)
            def _():
                far("item", to, cs.at[p, b], crd.at[b], csend.at[p, b], cdrecv.at[b]).start()

            @pl.when(to != p)
            def _():
                far("item", to, cs.at[p, b], cr.at[p, b], csend.at[p, b], crecv.at[p, b]).start()

    def chain(p, way):
        await_grads(p)

        def one(b, c):
            pass_on(p, b, way, False)
            return c
        lax.fori_loop(0, B, one, 0)

    def plane(d, way):
        return z - d if way == 0 else z + d

    def start_chain(d, way):
        out = 1 - way
        edge = z == 0 if out == 0 else z == Z - 1

        @pl.when(comes(d, way) & edge)
        def _():
            chain(plane(d, way), out)

    spread(z, items)
    compute(z)
    for d in range(1, Z):
        for way in (0, 1):
            @pl.when(comes(d, way))
            def _(d=d, way=way):
                zcopy(d, way).wait_recv()
                if d + 1 < Z:
                    pl.when(can_send(d + 1, way))(lambda: zcopy(d + 1, way).start())
                spread(plane(d, way), zbufs[2 * (d - 1) + way])
        for way in (0, 1):
            pl.when(comes(d, way))(lambda d=d, way=way: compute(plane(d, way)))
        if d + 1 < Z:
            for way in (0, 1):
                start_chain(d, way)

    def ucopy(to, src):
        return far("item", to, us.at[to], ur.at[src], usend.at[to], urecv.at[src])

    for j in range(1, Z):
        to = lax.rem(z + j, Z)
        encode(us.at[to], ug[pl.ds(pl.multiple_of(to * piece, piece), piece), :], user_unit)
        ucopy(to, z).start()
    for way in (0, 1):
        start_chain(Z - 1, way)

    def vcopy(to, src, j):
        return far("item", to, ugs, ugr.at[src], vsend.at[j], vrecv.at[src])

    def share_users():
        total = ug[pl.ds(pl.multiple_of(z * piece, piece), piece), :]
        for j in range(1, Z):
            src = lax.rem(z + j, Z)
            ucopy(z, src).wait_recv()
            total = total + decode(ur.at[src], user_unit)
        encode(ugs, total, user_unit)
        for j in range(1, Z):
            vcopy(lax.rem(z + j, Z), z, j - 1).start()
        user_out[pl.ds(pl.multiple_of(z * piece, piece), piece), :] = decode(ugs, user_unit)

    inner = (z > 0) & (z < Z - 1)
    pl.when(inner)(lambda: [await_grads(lax.rem(z + j, Z)) for j in range(1, Z)] and None)

    def relay(r):
        def up(b):
            pl.when(z < r)(lambda: pass_on(r, b, 0, True))

        def down(b):
            pl.when(z > Z - 1 - r)(lambda: pass_on(Z - 1 - r, b, 1, True))

        def one(b, c):
            pl.when(2 * z < Z - 1)(lambda: up(b))
            down(b)
            pl.when(2 * z >= Z - 1)(lambda: up(b))
            return c
        lax.fori_loop(0, B, one, 0)

    for r in range(1, Z - 1):
        pl.when(inner)(lambda r=r: relay(r))
    pl.when(inner)(lambda: relay(Z - 1))
    share_users()

    await_grads(z)

    def finish(b, c):
        item_out[b] = dense(z, b)

        @pl.when(z > 0)
        def _():
            far("item", z, cs.at[z, b], cr.at[z, b], csend.at[z, b], crecv.at[z, b]).wait_recv()
            item_out[b] += decode(cr.at[z, b], item_unit)

        @pl.when(z < Z - 1)
        def _():
            far("item", z, cs.at[z, b], crd.at[b], csend.at[z, b], cdrecv.at[b]).wait_recv()
            item_out[b] += decode(crd.at[b], item_unit)
        return c

    lax.fori_loop(0, B, finish, 0)

    for j in range(1, Z):
        src = lax.rem(z + j, Z)
        vcopy(z, src, j - 1).wait_recv()
        user_out[pl.ds(pl.multiple_of(src * piece, piece), piece), :] = decode(ugr.at[src], user_unit)

    for d in range(1, Z):
        for way in (0, 1):
            pl.when(can_send(d, way))(lambda d=d, way=way: zcopy(d, way).wait_send())

    def drain(j, c):
        to = lax.rem(me + j, U)
        for p in range(Z):
            icopy(p, to, me).wait_send()
            gcopy(p, to, me).wait_send()
        return c

    lax.fori_loop(1, U, drain, 0)
    for j in range(1, Z):
        to = lax.rem(z + j, Z)
        ucopy(to, z).wait_send()
        vcopy(to, z, j - 1).wait_send()

        def drained(b, c):
            far("item", z, cs.at[to, b], cr.at[to, b], csend.at[to, b], crecv.at[to, b]).wait_send()
            return c
        lax.fori_loop(0, B, drained, 0)


def exchange(pick, items, user, feedback, U, Z):
    B, T, K = items.shape
    N = user.shape[0]
    piece = N // Z
    coded = T + PAD
    dma = pltpu.SemaphoreType.DMA
    i16 = jnp.int16
    vmem = pl.BlockSpec(memory_space=pltpu.VMEM)
    return pl.pallas_call(
        functools.partial(kernel, U, Z),
        out_shape=(jax.ShapeDtypeStruct((B, T, K), jnp.float32), jax.ShapeDtypeStruct((N, K), jnp.float32)),
        in_specs=[pl.BlockSpec(memory_space=pltpu.SMEM), vmem, vmem, pl.BlockSpec(memory_space=pl.ANY)],
        out_specs=(vmem, vmem),
        scratch_shapes=[pltpu.VMEM((B, T, K), jnp.bfloat16)] * (2 * (Z - 1) + 1) + [
            pltpu.VMEM((N, K), jnp.bfloat16),
            pltpu.VMEM((Z, U, T, K), jnp.bfloat16),
            pltpu.VMEM((Z, U, T, K), jnp.bfloat16),
            pltpu.VMEM((Z, U, coded, K), i16),
            pltpu.VMEM((Z, U, coded, K), i16),
            pltpu.VMEM((Z, B, coded, K), i16),
            pltpu.VMEM((Z, B, coded, K), i16),
            pltpu.VMEM((B, coded, K), i16),
            pltpu.VMEM((2, 2, N, T), jnp.bfloat16),
            pltpu.VMEM((Z, piece + PAD, K), i16),
            pltpu.VMEM((Z, piece + PAD, K), i16),
            pltpu.VMEM((piece + PAD, K), i16),
            pltpu.VMEM((Z, piece + PAD, K), i16),
            pltpu.VMEM((N, K), jnp.float32),
            dma((2 * (Z - 1),)), dma((2 * (Z - 1),)),
            dma((Z, U)), dma((Z, U)), dma((Z, U)), dma((Z, U)),
            dma((Z, B)), dma((Z, B)), dma((B,)),
            dma((2,)),
            dma((Z,)), dma((Z,)), dma((Z,)), dma((Z,)),
        ],
        compiler_params=pltpu.CompilerParams(
            collective_id=0, has_side_effects=True, vmem_limit_bytes=63 * 2**20),
    )(pick, items, user, feedback)


def local(user_factors, item_factors, feedback, item_pick, user_noise, item_noise):
    U, Z = lax.axis_size("user"), lax.axis_size("item")
    tile, rank = feedback.shape[2], item_factors.shape[1]
    held = item_factors.shape[0] // tile
    items = item_factors.reshape(held, tile, rank)
    item_grad, user_grad = exchange(
        item_pick, items, user_factors,
        feedback.reshape(U, Z, feedback.shape[1], tile), U, Z)
    item_grad = item_grad.reshape(item_factors.shape)
    new_item = item_factors - item_step * (item_grad + prior_weight * item_factors) + item_noise_scale * item_noise
    new_user = user_factors - step_size * (user_grad + prior_weight * user_factors) + noise_scale * user_noise
    return (new_user, new_item)


def solution(mesh):
    in_specs = (
        P("user", None),
        P(("user", "item"), None),
        P("item", "user", None),
        P(),
        P("user", None),
        P(("user", "item"), None),
    )
    out_specs = (P("user", None), P(("user", "item"), None))
    return jax.shard_map(local, mesh=mesh, in_specs=in_specs, out_specs=out_specs, check_vma=False)
```

```python
import functools
import math

import jax
import jax.numpy as jnp
from jax import lax
from jax.experimental import pallas as pl
from jax.experimental.pallas import tpu as pltpu
from jax.sharding import PartitionSpec as P

step_size = 0.01
item_step = 0.1
prior_weight = 1.0
noise_scale = math.sqrt(0.02)
item_noise_scale = math.sqrt(0.2)

FACTOR_BOUND = 1.5
LEVELS = 32766.0
RUN = 2
PAD = 8


def encode(ref, value, unit):
    rows = value.shape[0]
    largest = jnp.max(jnp.abs(value), axis=0, keepdims=True)
    count = jnp.floor(largest * (1.0 / (LEVELS * unit))) + 1.0
    inverse = 1.0 / (count * unit)
    ref[pl.ds(0, rows), :] = jnp.round(value * inverse).astype(jnp.int32).astype(jnp.int16)
    ref[pl.ds(rows, PAD), :] = jnp.broadcast_to(count, (PAD, value.shape[1])).astype(jnp.int32).astype(jnp.int16)


def decode(ref, weight):
    rows = ref.shape[0] - PAD
    count = ref[pl.ds(rows, PAD), :].astype(jnp.float32)[0:1]
    return ref[pl.ds(0, rows), :].astype(jnp.float32) * (count * weight)


def kernel(
    U, Z, pick, items_wide, user_wide, feedback, item_out, user_out, *scratch
):
    zbufs = scratch[: 2 * (Z - 1)]
    (items, user, og, arr, gs, gr, cs, cr, crd, fb, us, ur, ugs, ugr, ug, zsend, zrecv, isend, irecv, gsend, grecv,
     csend, crecv, cdrecv, fsem, usend, urecv, vsend, vrecv) = scratch[2 * (Z - 1):]
    B, T, K = items.shape
    N = user.shape[0]
    piece = N // Z
    me = lax.axis_index("user")
    z = lax.axis_index("item")
    item_unit = N * FACTOR_BOUND * U / LEVELS / 32000.0
    user_unit = U * Z * T * FACTOR_BOUND * Z / LEVELS / 32000.0

    def far(axis, to, src, dst, ssem, rsem):
        return pltpu.make_async_remote_copy(
            src_ref=src, dst_ref=dst, send_sem=ssem, recv_sem=rsem,
            device_id={axis: to}, device_id_type=pl.DeviceIdType.MESH)

    barrier = pltpu.get_barrier_semaphore()

    items[...] = items_wide[...].astype(jnp.bfloat16)

    def greet_user(j, c):
        pl.semaphore_signal(barrier, inc=1, device_id={"user": lax.rem(me + j, U)}, device_id_type=pl.DeviceIdType.MESH)
        return c

    lax.fori_loop(1, U, greet_user, 0)
    for j in range(1, Z):
        pl.semaphore_signal(barrier, inc=1, device_id={"item": lax.rem(z + j, Z)}, device_id_type=pl.DeviceIdType.MESH)
    pl.semaphore_wait(barrier, U - 1 + Z - 1)

    def zcopy(d, way):
        src = items if d == 1 else zbufs[2 * (d - 2) + way]
        k = 2 * (d - 1) + way
        return far("item", z + (1 if way == 0 else -1), src, zbufs[k], zsend.at[k], zrecv.at[k])

    def can_send(d, way):
        return (z - (d - 1) >= 0) & (z + 1 < Z) if way == 0 else (z + (d - 1) < Z) & (z >= 1)

    def comes(d, way):
        return z - d >= 0 if way == 0 else z + d < Z

    for way in (0, 1):
        pl.when(can_send(1, way))(lambda way=way: zcopy(1, way).start())

    user[...] = user_wide[...].astype(jnp.bfloat16)
    ug[...] = jnp.zeros_like(ug)

    def icopy(p, to, src):
        return far("user", to, og.at[p, to], arr.at[p, src], isend.at[p, to], irecv.at[p, src])

    def spread(p, blocks):
        def one(j, c):
            to = lax.rem(me + j, U)
            og[p, to] = blocks[pick[to * Z + z, me * Z + p]]
            icopy(p, to, me).start()
            return c
        lax.fori_loop(1, U, one, 0)
        arr[p, me] = blocks[pick[me * Z + z, me * Z + p]]

    def gcopy(p, to, src):
        return far("user", to, gs.at[p, to], gr.at[p, src], gsend.at[p, to], grecv.at[p, src])

    def fcopy(p, pair, slot):
        return pltpu.make_async_copy(feedback.at[pl.ds(2 * pair, 2), p], fb.at[slot], fsem.at[slot])

    pairs = U // 2

    def pair_of(j):
        return lax.rem(me // 2 + pairs - j, pairs)

    def compute(p):
        fcopy(p, pair_of(0), 0).start()

        def one(j, c):
            pair = pair_of(j)
            slot = lax.rem(j, 2)

            @pl.when(j + 1 < pairs)
            def _():
                fcopy(p, pair_of(j + 1), 1 - slot).start()

            for t in range(2):
                o = 2 * pair + t
                pl.when(o != me)(lambda o=o: icopy(p, me, o).wait_recv())
            fcopy(p, pair, slot).wait()
            tile = arr[p, pl.ds(2 * pair, 2)].reshape(2 * T, K)
            scores = lax.dot_general(user[...], tile, (((1,), (1,)), ((), ())), preferred_element_type=jnp.float32)
            target = jnp.concatenate([fb[slot, 0], fb[slot, 1]], axis=1).astype(jnp.float32)
            residual = (0.5 * jnp.tanh(0.5 * scores) + (0.5 - target)).astype(jnp.bfloat16)
            part = lax.dot_general(residual, user[...], (((0,), (0,)), ((), ())), preferred_element_type=jnp.float32)
            for t in range(2):
                o = 2 * pair + t
                value = part[t * T:(t + 1) * T]

                @pl.when(o != me)
                def _():
                    encode(gs.at[p, o], value, item_unit)
                    gcopy(p, o, me).start()

                @pl.when(o == me)
                def _():
                    encode(gr.at[p, me], value, item_unit)
            ug[...] += jnp.dot(residual, tile, preferred_element_type=jnp.float32)
            return c

        lax.fori_loop(0, pairs, one, 0)

    def dense(p, b):
        def one(u, acc):
            weight = jnp.where(pick[u * Z + z, me * Z + p] == b, item_unit, 0.0).astype(jnp.float32)
            return acc + decode(gr.at[p, u], weight)
        return lax.fori_loop(0, U, one, jnp.zeros((T, K), jnp.float32))

    def await_grads(p):
        def one(j, c):
            gcopy(p, me, lax.rem(me + j, U)).wait_recv()
            return c
        lax.fori_loop(1, U, one, 0)

    def run(b):
        return pl.ds(b * RUN, RUN)

    def up_copy(to, p, c):
        return far("item", to, cs.at[p, run(c)], cr.at[p, run(c)], csend.at[p, c], crecv.at[p, c])

    def last_copy(to, p, c):
        return far("item", to, cs.at[p, run(c)], crd.at[run(c)], csend.at[p, c], cdrecv.at[c])

    def pass_on(p, c, way, relay):
        to = z + (1 if way == 0 else -1)
        if relay:
            up_copy(z, p, c).wait_recv()

        def one(i, carry):
            b = c * RUN + i
            total = dense(p, b)
            if relay:
                total = total + decode(cr.at[p, b], item_unit)
            encode(cs.at[p, b], total, item_unit)
            return carry
        lax.fori_loop(0, RUN, one, 0)
        if way == 0:
            up_copy(to, p, c).start()
        else:
            pl.when(to == p)(lambda: last_copy(to, p, c).start())
            pl.when(to != p)(lambda: up_copy(to, p, c).start())

    def chain(p, way):
        await_grads(p)

        def one(c, carry):
            pass_on(p, c, way, False)
            return carry
        lax.fori_loop(0, B // RUN, one, 0)

    def plane(d, way):
        return z - d if way == 0 else z + d

    def start_chain(d, way):
        out = 1 - way
        edge = z == 0 if out == 0 else z == Z - 1

        @pl.when(comes(d, way) & edge)
        def _():
            chain(plane(d, way), out)

    spread(z, items)
    compute(z)
    for d in range(1, Z):
        for way in (0, 1):
            @pl.when(comes(d, way))
            def _(d=d, way=way):
                zcopy(d, way).wait_recv()
                if d + 1 < Z:
                    pl.when(can_send(d + 1, way))(lambda: zcopy(d + 1, way).start())
                spread(plane(d, way), zbufs[2 * (d - 1) + way])
        for way in (0, 1):
            pl.when(comes(d, way))(lambda d=d, way=way: compute(plane(d, way)))
        if d + 1 < Z:
            for way in (0, 1):
                start_chain(d, way)

    def ucopy(to, src):
        return far("item", to, us.at[to], ur.at[src], usend.at[to], urecv.at[src])

    for j in range(1, Z):
        to = lax.rem(z + j, Z)
        encode(us.at[to], ug[pl.ds(pl.multiple_of(to * piece, piece), piece), :], user_unit)
        ucopy(to, z).start()
    for way in (0, 1):
        start_chain(Z - 1, way)

    def vcopy(to, src, j):
        return far("item", to, ugs, ugr.at[src], vsend.at[j], vrecv.at[src])

    def share_users():
        total = ug[pl.ds(pl.multiple_of(z * piece, piece), piece), :]
        for j in range(1, Z):
            src = lax.rem(z + j, Z)
            ucopy(z, src).wait_recv()
            total = total + decode(ur.at[src], user_unit)
        encode(ugs, total, user_unit)
        for j in range(1, Z):
            vcopy(lax.rem(z + j, Z), z, j - 1).start()
        user_out[pl.ds(pl.multiple_of(z * piece, piece), piece), :] = decode(ugs, user_unit)

    inner = (z > 0) & (z < Z - 1)
    pl.when(inner)(lambda: [await_grads(lax.rem(z + j, Z)) for j in range(1, Z)] and None)

    def relay(r):
        def up(b):
            pl.when(z < r)(lambda: pass_on(r, b, 0, True))

        def down(b):
            pl.when(z > Z - 1 - r)(lambda: pass_on(Z - 1 - r, b, 1, True))

        def one(b, c):
            pl.when(2 * z < Z - 1)(lambda: up(b))
            down(b)
            pl.when(2 * z >= Z - 1)(lambda: up(b))
            return c
        lax.fori_loop(0, B // RUN, one, 0)

    for r in range(1, Z - 1):
        pl.when(inner)(lambda r=r: relay(r))
    pl.when(inner)(lambda: relay(Z - 1))
    share_users()

    await_grads(z)

    def finish(b, c):
        item_out[b] = dense(z, b)

        @pl.when(z > 0)
        def _():
            pl.when(lax.rem(b, RUN) == 0)(lambda: up_copy(z, z, b // RUN).wait_recv())
            item_out[b] += decode(cr.at[z, b], item_unit)

        @pl.when(z < Z - 1)
        def _():
            pl.when(lax.rem(b, RUN) == 0)(lambda: last_copy(z, z, b // RUN).wait_recv())
            item_out[b] += decode(crd.at[b], item_unit)
        return c

    lax.fori_loop(0, B, finish, 0)

    for j in range(1, Z):
        src = lax.rem(z + j, Z)
        vcopy(z, src, j - 1).wait_recv()
        user_out[pl.ds(pl.multiple_of(src * piece, piece), piece), :] = decode(ugr.at[src], user_unit)

    for d in range(1, Z):
        for way in (0, 1):
            pl.when(can_send(d, way))(lambda d=d, way=way: zcopy(d, way).wait_send())

    def drain(j, c):
        to = lax.rem(me + j, U)
        for p in range(Z):
            icopy(p, to, me).wait_send()
            gcopy(p, to, me).wait_send()
        return c

    lax.fori_loop(1, U, drain, 0)
    for j in range(1, Z):
        to = lax.rem(z + j, Z)
        ucopy(to, z).wait_send()
        vcopy(to, z, j - 1).wait_send()

        def drained(b, c):
            up_copy(z, to, b).wait_send()
            return c
        lax.fori_loop(0, B // RUN, drained, 0)


def exchange(pick, items, user, feedback, U, Z):
    B, T, K = items.shape
    N = user.shape[0]
    piece = N // Z
    coded = T + PAD
    dma = pltpu.SemaphoreType.DMA
    i16 = jnp.int16
    vmem = pl.BlockSpec(memory_space=pltpu.VMEM)
    return pl.pallas_call(
        functools.partial(kernel, U, Z),
        out_shape=(jax.ShapeDtypeStruct((B, T, K), jnp.float32), jax.ShapeDtypeStruct((N, K), jnp.float32)),
        in_specs=[pl.BlockSpec(memory_space=pltpu.SMEM), vmem, vmem, pl.BlockSpec(memory_space=pl.ANY)],
        out_specs=(vmem, vmem),
        scratch_shapes=[pltpu.VMEM((B, T, K), jnp.bfloat16)] * (2 * (Z - 1) + 1) + [
            pltpu.VMEM((N, K), jnp.bfloat16),
            pltpu.VMEM((Z, U, T, K), jnp.bfloat16),
            pltpu.VMEM((Z, U, T, K), jnp.bfloat16),
            pltpu.VMEM((Z, U, coded, K), i16),
            pltpu.VMEM((Z, U, coded, K), i16),
            pltpu.VMEM((Z, B, coded, K), i16),
            pltpu.VMEM((Z, B, coded, K), i16),
            pltpu.VMEM((B, coded, K), i16),
            pltpu.VMEM((2, 2, N, T), jnp.bfloat16),
            pltpu.VMEM((Z, piece + PAD, K), i16),
            pltpu.VMEM((Z, piece + PAD, K), i16),
            pltpu.VMEM((piece + PAD, K), i16),
            pltpu.VMEM((Z, piece + PAD, K), i16),
            pltpu.VMEM((N, K), jnp.float32),
            dma((2 * (Z - 1),)), dma((2 * (Z - 1),)),
            dma((Z, U)), dma((Z, U)), dma((Z, U)), dma((Z, U)),
            dma((Z, B // RUN)), dma((Z, B // RUN)), dma((B // RUN,)),
            dma((2,)),
            dma((Z,)), dma((Z,)), dma((Z,)), dma((Z,)),
        ],
        compiler_params=pltpu.CompilerParams(
            collective_id=0, has_side_effects=True, vmem_limit_bytes=63 * 2**20),
    )(pick, items, user, feedback)


def local(user_factors, item_factors, feedback, item_pick, user_noise, item_noise):
    U, Z = lax.axis_size("user"), lax.axis_size("item")
    tile, rank = feedback.shape[2], item_factors.shape[1]
    held = item_factors.shape[0] // tile
    items = item_factors.reshape(held, tile, rank)
    item_grad, user_grad = exchange(
        item_pick, items, user_factors,
        feedback.reshape(U, Z, feedback.shape[1], tile), U, Z)
    item_grad = item_grad.reshape(item_factors.shape)
    new_item = item_factors - item_step * (item_grad + prior_weight * item_factors) + item_noise_scale * item_noise
    new_user = user_factors - step_size * (user_grad + prior_weight * user_factors) + noise_scale * user_noise
    return (new_user, new_item)


def solution(mesh):
    in_specs = (
        P("user", None),
        P(("user", "item"), None),
        P("item", "user", None),
        P(),
        P("user", None),
        P(("user", "item"), None),
    )
    out_specs = (P("user", None), P(("user", "item"), None))
    return jax.shard_map(local, mesh=mesh, in_specs=in_specs, out_specs=out_specs, check_vma=False)
```
